512 devices in a mesh: pipe: 8 (over x, core), expert: 64 (over z, y).
Axes of the slice: x: 4, y: 4, z: 16, core: 2. Of those that a mesh axis runs over, the one named last changes fastest.
Arguments:
- inputs: bfloat16 [8, 8192, 2048], P('pipe', 'expert'), may hold values from -6 to 6
- out_grads: bfloat16 [8, 8192, 2048], P('pipe', 'expert'), may hold values from -6 to 6
- expert_ids: int32 [8, 8192, 8], P('pipe', 'expert'), may hold values from 0 to 127, all different within a row
- gate_values: float32 [8, 8192, 8], P('pipe', 'expert'), may hold values from 0.2 to 1
- w_gate: bfloat16 [8, 2048, 16384], P('pipe', None, 'expert'), may hold values from -0.125 to 0.125
- w_up: bfloat16 [8, 2048, 16384], P('pipe', None, 'expert'), may hold values from -0.125 to 0.125
- w_down: bfloat16 [8, 16384, 2048], P('pipe', 'expert'), may hold values from -0.1875 to 0.1875
Outputs:
- prev_grads: bfloat16 [8, 8192, 2048], P('pipe', 'expert')
- gate_grads: float32 [8, 8192, 8], P('pipe', 'expert')
The draws below stay inside these ranges and needn't reach their ends.
Inputs may be any that keep to these rules, and one draw needn't show every extreme that they name: `expert_ids`: each token names 8 different experts.
All inputs are finite; a program needn't handle non-finite values.
Results may differ from the reference program's by a relative error of at most 0.0057.
Values may be sent and summed in bfloat16 or wider, within the bound.
A program may use at most 64 MiB of HBM per device.

```python
import jax
import jax.numpy as jnp
from jax import lax

D = 2048
FF = 1024
EXPERTS_ALL = 128
TOPK = 8
SLICES = 4
TOK_DEV = 128
CAP = 12
EXP_FLIGHT = 16
SECTIONS = 8
TOKENS = 8192
N_EXPERT = 64


def steps_of(rng, dims, cuts, low, high):
    def one(dim, shards_of):
        steps = jax.random.uniform(jax.random.fold_in(jax.random.fold_in(rng, 6), dim), (shards_of,), jnp.float32, low / len(cuts), high / len(cuts))
        return jnp.repeat(jnp.exp(steps), dims[dim] // shards_of).reshape((-1,) + (1,) * (len(dims) - dim - 1))

    level = one(*cuts[0])
    for cut in cuts[1:]:
        level = level * one(*cut)
    return level


def different_ones(own_key, rows, amount, top, lift):
    ranking = jax.random.permutation(jax.random.fold_in(own_key, 1), amount)
    favour = ranking
    for power in range(3):
        favour = favour * favour // amount
    favour = favour * lift // amount
    tickets = jax.random.randint(jax.random.fold_in(own_key, 2), (rows, amount), 0, 4096) + favour
    holders = jax.random.permutation(jax.random.fold_in(own_key, 3), rows)[jnp.arange(amount) % rows]
    tickets = jnp.where(jnp.arange(rows)[:, None] == holders[None, :], 1 << 14, tickets)
    priority = tickets * amount + jnp.arange(amount)
    return lax.top_k(priority.astype(jnp.int32), top)[1].astype(jnp.int32)


def centred(stream_key, extent, spread, most, cuts=(), kind=jnp.bfloat16):
    entries = spread * jax.random.normal(stream_key, extent, jnp.float32)
    if cuts:
        entries = entries * steps_of(stream_key, extent, cuts, -0.22, 0.18)
    return jnp.clip(entries, -most, most).astype(kind)


def setup_inputs(seed: int = 0) -> dict:
    splits = jax.random.split(jax.random.key(seed), 8)
    return {
        "inputs": centred(splits[0], (SECTIONS, TOKENS, D), 1.0, 6.0, ((0, 8), (1, 64))),
        "out_grads": centred(splits[1], (SECTIONS, TOKENS, D), 1.0, 6.0, ((0, 8), (1, 64))),
        "expert_ids": different_ones(splits[2], SECTIONS * TOKENS, EXPERTS_ALL, TOPK, 1024).reshape((SECTIONS, TOKENS, TOPK)),
        "gate_values": jnp.clip(0.2 + 0.8 * jax.random.uniform(splits[3], (SECTIONS, TOKENS, TOPK), jnp.float32) ** steps_of(splits[3], (SECTIONS, TOKENS, TOPK), ((0, 8), (1, 64)), -0.2, 0.2), 0.2, 1.0),
        "w_gate": centred(splits[4], (SECTIONS, D, EXP_FLIGHT * FF), D ** -0.5, 0.125, ((0, 8), (2, 64))),
        "w_up": centred(splits[5], (SECTIONS, D, EXP_FLIGHT * FF), D ** -0.5, 0.125, ((0, 8), (2, 64))),
        "w_down": centred(splits[6], (SECTIONS, EXP_FLIGHT * FF, D), FF ** -0.5, 0.1875, ((0, 8), (1, 64))),
    }


def expert_grads(rows_in, rows_grad, gate_cols, up_cols, down_rows):
    gate_pre = jnp.dot(rows_in, gate_cols, preferred_element_type=jnp.float32)
    up_pre = jnp.dot(rows_in, up_cols, preferred_element_type=jnp.float32)
    sig = jax.nn.sigmoid(gate_pre)
    act = gate_pre * sig
    hidden = act * up_pre
    dhidden = jnp.dot(rows_grad, down_rows.T, preferred_element_type=jnp.float32)
    gate_part = jnp.sum(hidden * dhidden, axis=1)
    d_gate_pre = (dhidden * up_pre * sig * (1.0 + gate_pre * (1.0 - sig))).astype(jnp.bfloat16)
    d_up_pre = (dhidden * act).astype(jnp.bfloat16)
    back = jnp.dot(d_gate_pre, gate_cols.T, preferred_element_type=jnp.float32)
    back = back + jnp.dot(d_up_pre, up_cols.T, preferred_element_type=jnp.float32)
    return back, gate_part


def section_grads(tokens, grads, ids, gates, w_gate, w_up, w_down):
    blocks = N_EXPERT
    flight = N_EXPERT // SLICES
    tok = tokens.reshape(blocks, TOK_DEV, D)
    grd = grads.reshape(blocks, TOK_DEV, D)
    idb = ids.reshape(blocks, TOK_DEV, TOPK)
    gtb = gates.reshape(blocks, TOK_DEV, TOPK)
    experts_here = jnp.arange(flight, dtype=jnp.int32)
    match = idb[:, :, :, None] == experts_here[None, None, None, :]
    routed = jnp.sum(match.astype(jnp.int32), axis=2)
    weight_te = jnp.sum(jnp.where(match, gtb[:, :, :, None], jnp.float32(0.0)), axis=2)
    before = jnp.cumsum(routed, axis=1) - routed
    kept = (routed > 0) & (before < CAP)
    slots = jnp.arange(CAP, dtype=jnp.int32)
    keptt = jnp.transpose(kept, (0, 2, 1))
    beforet = jnp.transpose(before, (0, 2, 1))
    place = (keptt[:, :, None, :] & (beforet[:, :, None, :] == slots[None, None, :, None])).astype(jnp.float32)
    rows_x = jnp.einsum('bect,btd->ebcd', place, tok.astype(jnp.float32)).astype(jnp.bfloat16)
    rows_g = jnp.einsum('bect,btd->ebcd', place, grd.astype(jnp.float32)).astype(jnp.bfloat16)
    width_dev = FF // SLICES

    def one_expert(e):
        flat_x = rows_x[e].reshape(blocks * CAP, D)
        flat_g = rows_g[e].reshape(blocks * CAP, D)
        back_sum = jnp.zeros((blocks * CAP, D), jnp.float32)
        part_sum = jnp.zeros((blocks * CAP,), jnp.float32)
        for piece in range(SLICES):
            start = (e * FF + piece * width_dev).astype(jnp.int32)
            gate_cols = lax.dynamic_slice_in_dim(w_gate, start, width_dev, 1)
            up_cols = lax.dynamic_slice_in_dim(w_up, start, width_dev, 1)
            down_rows = lax.dynamic_slice_in_dim(w_down, start, width_dev, 0)
            back, part = expert_grads(flat_x, flat_g, gate_cols, up_cols, down_rows)
            back_bf = lax.optimization_barrier(back.astype(jnp.bfloat16))
            part_bf = lax.optimization_barrier(part.astype(jnp.bfloat16))
            back_sum = back_sum + back_bf.astype(jnp.float32)
            part_sum = part_sum + part_bf.astype(jnp.float32)
        return back_sum.reshape(blocks, CAP, D), part_sum.reshape(blocks, CAP)

    total, gsum = lax.map(one_expert, experts_here)
    mix = place * jnp.transpose(weight_te, (0, 2, 1))[:, :, None, :]
    moe = jnp.einsum('bect,ebcd->btd', mix, total, precision=lax.Precision.HIGHEST)
    d_gate_te = jnp.einsum('bect,ebc->bte', place, gsum, precision=lax.Precision.HIGHEST)
    d_gates = jnp.sum(jnp.where(match, d_gate_te[:, :, None, :], jnp.float32(0.0)), axis=3)
    return moe.astype(jnp.bfloat16).reshape(TOKENS, D), d_gates.reshape(TOKENS, TOPK)


def reference(inputs, out_grads, expert_ids, gate_values, w_gate, w_up, w_down):
    moes = []
    gradg = []
    for section in range(SECTIONS):
        moe, dg = section_grads(inputs[section], out_grads[section], expert_ids[section], gate_values[section], w_gate[section], w_up[section], w_down[section])
        moes.append(moe)
        gradg.append(dg)
    moe_all = jnp.stack(moes, axis=0)
    prev_grads = jnp.concatenate([moe_all[1:], moe_all[:1]], axis=0)
    return prev_grads, jnp.stack(gradg, axis=0)
```

```python
import jax
import jax.numpy as jnp
from jax import lax
from jax.sharding import PartitionSpec as P

SLICES = 4
CAP = 12


def shifted(block, axis, distance):
    devices = range(lax.axis_size(axis))
    route = [((i - distance) % len(devices), i) for i in devices]
    return lax.ppermute(block, axis, route)


def expert_grads(rows_in, rows_grad, gate_cols, up_cols, down_rows):
    gate_pre = jnp.dot(rows_in, gate_cols, preferred_element_type=jnp.float32)
    up_pre = jnp.dot(rows_in, up_cols, preferred_element_type=jnp.float32)
    sig = jax.nn.sigmoid(gate_pre)
    act = gate_pre * sig
    hidden = act * up_pre
    dhidden = lax.dot_general(
        rows_grad, down_rows, (((1,), (1,)), ((), ())), preferred_element_type=jnp.float32
    )
    gate_part = jnp.sum(hidden * dhidden, axis=1)
    d_gate_pre = (dhidden * up_pre * sig * (1.0 + gate_pre * (1.0 - sig))).astype(jnp.bfloat16)
    d_up_pre = (dhidden * act).astype(jnp.bfloat16)
    back = lax.dot_general(
        d_gate_pre, gate_cols, (((1,), (1,)), ((), ())), preferred_element_type=jnp.float32
    )
    back = back + lax.dot_general(
        d_up_pre, up_cols, (((1,), (1,)), ((), ())), preferred_element_type=jnp.float32
    )
    return (back, gate_part)


def along_z():
    planes = lax.axis_size("expert") // SLICES
    return [[z * SLICES + y for z in range(planes)] for y in range(SLICES)]


def along_y():
    planes = lax.axis_size("expert") // SLICES
    return [[z * SLICES + y for y in range(SLICES)] for z in range(planes)]


def swap(block, groups):
    return lax.all_to_all(
        block, "expert", split_axis=0, concat_axis=0, tiled=True, axis_index_groups=groups
    )


def per_device(inputs, out_grads, expert_ids, gate_values, w_gate, w_up, w_down):
    devices_axis = lax.axis_size("expert")
    flight = devices_axis // SLICES
    tokens = inputs[0]
    grads = out_grads[0]
    ids = expert_ids[0]
    gates = gate_values[0]
    gate_cols = w_gate[0]
    up_cols = w_up[0]
    down_rows = w_down[0]
    count = tokens.shape[0]
    width = tokens.shape[1]
    experts_here = jnp.arange(flight, dtype=jnp.int32)
    match = ids[:, :, None] == experts_here[None, None, :]
    routed = jnp.sum(match.astype(jnp.int32), axis=1)
    weight_te = jnp.sum(jnp.where(match, gates[:, :, None], jnp.float32(0.0)), axis=1)
    before = jnp.cumsum(routed, axis=0) - routed
    kept = (routed > 0) & (before < CAP)
    slots = jnp.arange(CAP, dtype=jnp.int32)
    place = kept.T[:, None, :] & (before.T[:, None, :] == slots[None, :, None])
    place_bf = place.astype(jnp.bfloat16)
    send_x = jnp.einsum("ect,td->ecd", place_bf, tokens, preferred_element_type=jnp.float32).astype(
        jnp.bfloat16
    )
    send_g = jnp.einsum("ect,td->ecd", place_bf, grads, preferred_element_type=jnp.float32).astype(
        jnp.bfloat16
    )
    send = jnp.concatenate([send_x, send_g], axis=1)
    mine = swap(send, along_z())
    rows = lax.all_gather(mine, "expert", axis_index_groups=along_y(), axis=0, tiled=False)
    rows = rows.reshape(devices_axis, 2 * CAP, width)
    back, part = expert_grads(
        rows[:, :CAP].reshape(devices_axis * CAP, width),
        rows[:, CAP:].reshape(devices_axis * CAP, width),
        gate_cols,
        up_cols,
        down_rows,
    )
    back_bf = back.astype(jnp.bfloat16).reshape(SLICES, flight * CAP, width)
    part_bf = part.astype(jnp.bfloat16).reshape(SLICES, flight * CAP)
    parts = swap(back_bf, along_y())
    qparts = swap(part_bf, along_y())
    summed = jnp.sum(parts.astype(jnp.float32), axis=0).astype(jnp.bfloat16)
    qsum = jnp.sum(qparts.astype(jnp.float32), axis=0)
    total = swap(summed.reshape(flight, CAP, width), along_z()).astype(jnp.float32)
    gsum = swap(qsum.reshape(flight, CAP), along_z())
    place_f = place.astype(jnp.float32)
    mix = jnp.transpose(place_f * weight_te.T[:, None, :], (2, 0, 1)).reshape(count, flight * CAP)
    moe = jnp.dot(
        mix,
        total.reshape(flight * CAP, width),
        precision=lax.Precision.HIGHEST,
        preferred_element_type=jnp.float32,
    )
    moe_bf = moe.astype(jnp.bfloat16)
    d_gate_te = jnp.einsum("ect,ec->te", place_f, gsum, precision=lax.Precision.HIGHEST)
    d_gates = jnp.sum(jnp.where(match, d_gate_te[:, None, :], jnp.float32(0.0)), axis=2)
    arrived = shifted(moe_bf, "pipe", -1)
    return (arrived[None], d_gates[None])


def solution(mesh):
    return jax.shard_map(
        per_device,
        mesh=mesh,
        in_specs=(
            P("pipe", "expert", None),
            P("pipe", "expert", None),
            P("pipe", "expert", None),
            P("pipe", "expert", None),
            P("pipe", None, "expert"),
            P("pipe", None, "expert"),
            P("pipe", "expert", None),
        ),
        out_specs=(P("pipe", "expert", None), P("pipe", "expert", None)),
        check_vma=False,
    )
```
